512 devices in a mesh: chain: 8 (over x, core), tile: 64 (over y, z).
Axes of the slice: x: 4, y: 8, z: 8, core: 2. Of those that a mesh axis runs over, the one named last changes fastest.
Arguments:
- right_side: float32 [3, 2, 32, 32768], P(None, None, None, ('chain', 'tile')), may hold values from -6 to 6
- diag_inverse: float32 [2, 32768, 4096], P(None, ('chain', 'tile'))
- coupling: float32 [2, 32768, 4096], P(None, ('chain', 'tile')), may hold values from -0.0390625 to 0.0390625
- updates: float32 [131072, 192], P(('chain', 'tile')), may hold values from -2.4 to 2.4
- update_rows: int32 [131072], P(('chain', 'tile')), may hold values from 0 to 4095, as said below
- tile_counts: int32 [1024], P(('chain', 'tile')), may hold values from 32 to 128, as said below
Outputs:
- solution: float32 [3, 2, 32, 32768], P(None, None, None, ('chain', 'tile'))
The draws below stay inside these ranges and needn't reach their ends.
Inputs may be any that keep to these rules, and one draw needn't show every extreme that they name: `update_rows`: rows are counted within the supernode of the group that holds the entry. In each aligned block of 256 entries (the update rows of one device) at most 8 entries fall in any one aligned range of 64 rows, and in each run of 64 aligned blocks one such range receives exactly 8 entries from every block of the run. Padding rows carry entries too. `tile_counts`: one tile has all 128 rows live.
All inputs are finite; a program needn't handle non-finite values.
Results may differ from the reference program's by a relative error of at most 0.0001.
Values sent between devices are 32-bit elements; how exact they have to be, the bound alone decides.
A program may use at most 64 MiB of HBM per device.

```python
import math
import jax
import jax.numpy as jnp
from jax import lax

S = 4096
R = 32
NB = 3
UT = 2
TR = 128
NSUP = 8
GROUP = 64
BR = 64
CAP = 8


def draw_diag_inverse(key, part):
    total_rows = NSUP * S
    local_row = (jnp.arange(total_rows, dtype=jnp.int32) % S)[:, None]
    column = jnp.arange(S, dtype=jnp.int32)[None, :]
    spread = jax.random.normal(jax.random.fold_in(key, 31), (2, total_rows, S), jnp.float32) * (0.6 / math.sqrt(S))
    real_diag = jax.random.uniform(jax.random.fold_in(key, 32), (total_rows, 1), jnp.float32, 0.8, 1.4)
    imag_diag = jax.random.uniform(jax.random.fold_in(key, 33), (total_rows, 1), jnp.float32, -0.3, 0.3)
    diag_vals = jnp.stack([real_diag, imag_diag], axis=0)
    lower = jnp.where((column < local_row)[None, :, :], spread, 0.0)
    return lower + jnp.where((column == local_row)[None, :, :], diag_vals, 0.0)


def draw_update_rows(key, part):
    devices_all = NSUP * GROUP
    per_device = UT * TR
    slot_total = GROUP * CAP
    hot_owner = jax.random.randint(jax.random.fold_in(key, 11), (NSUP,), 0, GROUP)
    hot_device = jnp.repeat(hot_owner, GROUP)
    scores = jax.random.randint(jax.random.fold_in(key, 12), (devices_all, slot_total), 0, 1 << 20)
    slot_ids = jnp.arange(slot_total, dtype=jnp.int32)[None, :]
    scores = jnp.where(slot_ids // CAP == hot_device[:, None], -1 - slot_ids, scores)
    chosen = jnp.argsort(scores, axis=1, stable=True)[:, :per_device]
    owners = (chosen // CAP).astype(jnp.int32)
    shuffle_keys = jax.random.split(jax.random.fold_in(key, 13), devices_all)
    shuffles = jax.vmap(lambda single: jax.random.permutation(single, per_device))(shuffle_keys)
    owners = jnp.take_along_axis(owners, shuffles, axis=1)
    local_rows = jax.random.randint(jax.random.fold_in(key, 14), (devices_all, per_device), 0, BR)
    return (owners * BR + local_rows).reshape(-1).astype(jnp.int32)


def draw_tile_counts(key, part):
    tiles_all = NSUP * GROUP * UT
    counts = jax.random.randint(jax.random.fold_in(key, 21), (tiles_all,), TR // 4, TR + 1)
    full_tile = jax.random.randint(jax.random.fold_in(key, 22), (), 0, tiles_all)
    return jnp.where(jnp.arange(tiles_all, dtype=jnp.int32) == full_tile, TR, counts).astype(jnp.int32)


def shard_levels(stream_key, dims, cuts, least, top_value):
    factor_of = 1.0
    for dim, shards_of in cuts:
        heights = jax.random.uniform(jax.random.fold_in(jax.random.fold_in(stream_key, 6), dim), (shards_of,), jnp.float32, least / len(cuts), top_value / len(cuts))
        factor_of = factor_of * jnp.repeat(jnp.exp(heights), dims[dim] // shards_of).reshape((-1,) + (1,) * (len(dims) - 1 - dim))
    return factor_of


def bell_draw(key, shape, deviation, most, cuts=(), kind=jnp.bfloat16):
    result = deviation * jax.random.normal(key, shape, jnp.float32)
    if cuts:
        result = result * shard_levels(key, shape, cuts, -0.22, 0.18)
    return jnp.clip(result, -most, most).astype(kind)


def setup_inputs(seed: int = 0) -> dict:
    splits = jax.random.split(jax.random.key(seed), 7)
    return {
        "right_side": bell_draw(splits[0], (NB, 2, R, NSUP * S), 1.0, 6.0, ((3, 512),), jnp.float32),
        "diag_inverse": draw_diag_inverse(jax.random.fold_in(splits[6], 71), 0),
        "coupling": bell_draw(splits[2], (2, NSUP * S, S), (6 * S) ** -0.5, 0.0390625, ((1, 512),), jnp.float32),
        "updates": bell_draw(splits[3], (NSUP * GROUP * UT * TR, NB * 2 * R), 0.4, 2.4, ((0, 512),), jnp.float32),
        "update_rows": draw_update_rows(jax.random.fold_in(splits[6], 71), 0),
        "tile_counts": draw_tile_counts(jax.random.fold_in(splits[6], 71), 0),
    }


def complex_apply(matrix, reduced):
    products = jnp.einsum('bjrs,kis->bkjri', reduced, matrix, precision=lax.Precision.HIGHEST)
    real_part = products[:, 0, 0] - products[:, 1, 1]
    imag_part = products[:, 0, 1] + products[:, 1, 0]
    return jnp.stack([real_part, imag_part], axis=1)


def reference(right_side, diag_inverse, coupling, updates, update_rows, tile_counts):
    count_rows = updates.shape[0]
    row_index = jnp.arange(count_rows, dtype=jnp.int32)
    limits = jnp.repeat(tile_counts, TR)
    is_live = (row_index % TR) < limits
    live_updates = jnp.where(is_live[:, None], updates, jnp.zeros_like(updates))
    group_of = row_index // (GROUP * UT * TR)
    target = (group_of * S + update_rows).astype(jnp.int32)
    accumulated = jax.ops.segment_sum(live_updates, target, num_segments=NSUP * S)
    arranged = accumulated.reshape(NSUP * S, NB, 2, R).transpose(1, 2, 3, 0)
    reduced_all = right_side - arranged
    carried = jnp.zeros((NB, 2, R, S), jnp.float32)
    pieces = []
    for chain_step in range(NSUP):
        offset = chain_step * S
        reduced = reduced_all[:, :, :, offset:offset + S] - carried
        pieces.append(complex_apply(diag_inverse[:, offset:offset + S, :], reduced))
        carried = complex_apply(coupling[:, offset:offset + S, :], reduced)
    return jnp.concatenate(pieces, axis=3)
```

```python
import functools

import jax
import jax.numpy as jnp
from jax import lax
from jax.experimental import pallas as pl
from jax.experimental.pallas import tpu as pltpu
from jax.sharding import PartitionSpec as P

MESH = pl.DeviceIdType.MESH
F32 = jnp.float32
BF16 = jnp.bfloat16
SIDE = 8
SLOTS = 8
LANES = 128


def remote(src, dst, send_sem, recv_sem, device):
    return pltpu.make_async_remote_copy(
        src_ref=src, dst_ref=dst, send_sem=send_sem, recv_sem=recv_sem, device_id=device, device_id_type=MESH
    )


def split(value):
    high = value.astype(BF16)
    return high, (value - high.astype(F32)).astype(BF16)


def iota(shape, axis):
    return lax.broadcasted_iota(jnp.int32, shape, axis)


def kernel(chains, rhs, upd, rows, counts, diag, coup, out, wide, slots_out, slots_in, first, second,
           first_hi, first_lo, second_hi, second_lo, base, zbuf, part_in, part_out, diag_in, diag_out, stack,
           local_sem, slot_send, slot_recv, mat_send, mat_recv, z_send, z_recv, y_send, y_recv, d_send, d_recv):
    pieces, fold_rows = rhs.shape[0], rhs.shape[1]
    own = 2 * fold_rows
    group = SIDE * SIDE
    span = SIDE * own
    chain = lax.axis_index("chain")
    me = lax.axis_index("tile")
    y, z = me // SIDE, me % SIDE
    not_last = chain < chains - 1
    last = chain == chains - 1

    barrier = pltpu.get_barrier_semaphore()

    def greet(offset, carry):
        pl.semaphore_signal(barrier, inc=1, device_id=(chain, (me + offset) % group), device_id_type=MESH)
        return carry

    lax.fori_loop(1, group, greet, 0)

    @pl.when(not_last)
    def _():
        for row in range(SIDE):
            pl.semaphore_signal(barrier, inc=1, device_id=(chain + 1, row * SIDE + z), device_id_type=MESH)

    @pl.when(chain > 0)
    def _():
        for row in range(SIDE):
            pl.semaphore_signal(barrier, inc=1, device_id=(chain - 1, row * SIDE + z), device_id_type=MESH)

    count_rows = upd.shape[0]
    columns = upd.shape[1]
    wide[...] = jnp.zeros_like(wide)
    wide[:, :columns] = upd[...]
    row_of = rows[...]
    owner = lax.div(row_of, own)
    local = (row_of - owner * own).astype(F32)
    lane = iota((1, count_rows), 1)
    half = count_rows // 2
    live = jnp.where(lane < half, lane, lane - half) < jnp.where(lane < half, counts[0], counts[1])
    hits = (iota((group, count_rows), 0) == owner).astype(F32)
    before = (iota((count_rows, count_rows), 0) < iota((count_rows, count_rows), 1)).astype(F32).astype(BF16)
    earlier = jnp.dot(hits.astype(BF16), before, preferred_element_type=F32)
    rank = jnp.sum(hits * earlier, axis=0, keepdims=True)
    slot = jnp.where(live, owner.astype(F32) * SLOTS + rank, -1.0)
    pick = iota((group * SLOTS, count_rows), 0).astype(F32) == slot
    place = jnp.sum(jnp.where(pick, local, 0.0), axis=1, keepdims=True)
    pick = pick.astype(F32).astype(BF16)
    high, low = split(wide[...])
    payload = jnp.dot(pick, high, preferred_element_type=F32) + jnp.dot(pick, low, preferred_element_type=F32)
    payload = jnp.where(iota(payload.shape, 1) == columns, place, payload)
    slots_out[...] = payload.reshape(slots_out.shape)

    ends = (chain == 0) | last

    @pl.when(ends)
    def _():
        pl.semaphore_wait(barrier, group - 1 + SIDE)

    @pl.when(jnp.logical_not(ends))
    def _():
        pl.semaphore_wait(barrier, group - 1 + 2 * SIDE)

    def send_slots(offset, carry):
        peer = (me + offset) % group
        remote(slots_out.at[peer], slots_in.at[me], slot_send, slot_recv, (chain, peer)).start()
        return carry

    lax.fori_loop(1, group, send_slots, 0)
    slots_in[me] = slots_out[me]

    def columns_of(source, row):
        return source.at[:, :, pl.ds(pl.multiple_of(row * span, span), span)]

    def send_matrix(source, target, which):
        pltpu.make_async_copy(columns_of(source, y), target.at[y], local_sem.at[which]).start()
        for offset in (4, 3, 5, 2, 6, 1, 7):
            row = (y + offset) % SIDE
            remote(columns_of(source, row), target.at[y], mat_send.at[which], mat_recv.at[which],
                   (chain, row * SIDE + z)).start()

    def take_matrix(source, target, which, hi, lo):
        pltpu.make_async_copy(columns_of(source, y), target.at[y], local_sem.at[which]).wait()
        seven = target.at[pl.ds(0, SIDE - 1)]
        remote(seven, seven, mat_send.at[which], mat_recv.at[which], (chain, me)).wait_recv()

        def cut(row, carry):
            for part in range(2):
                high, low = split(target[row, part])
                at = pl.ds(pl.multiple_of(row * own, own), own)
                hi[at, part * span:(part + 1) * span] = high
                lo[at, part * span:(part + 1) * span] = low
            return carry

        lax.fori_loop(0, SIDE, cut, 0)

    @pl.when(not_last)
    def _():
        send_matrix(coup, first, 0)

    @pl.when(last)
    def _():
        send_matrix(diag, first, 0)

    most = slots_in.at[pl.ds(0, group - 1)]
    remote(most, most, slot_send, slot_recv, (chain, me)).wait_recv()
    arrived = slots_in[...].reshape(group * SLOTS, slots_in.shape[2])
    pick = (arrived[:, columns:columns + 1] == iota((group * SLOTS, own), 1).astype(F32)).astype(F32).astype(BF16)
    high, low = split(arrived)
    across = (((0,), (0,)), ((), ()))
    total = (lax.dot_general(pick, high, across, preferred_element_type=F32)
             + lax.dot_general(pick, low, across, preferred_element_type=F32))
    left = iota((fold_rows, LANES), 1) < LANES // 2
    for piece in range(pieces):
        tile = total[:, (piece // 2) * LANES:(piece // 2 + 1) * LANES]
        top, bottom = tile[:fold_rows], tile[fold_rows:]
        if piece % 2 == 0:
            folded = jnp.where(left, top, pltpu.roll(bottom, LANES // 2, 1))
        else:
            folded = jnp.where(left, pltpu.roll(top, LANES // 2, 1), bottom)
        base[piece] = rhs[piece] - folded

    take_matrix(coup, first, 0, first_hi, first_lo)

    @pl.when(not_last)
    def _():
        send_matrix(diag, second, 1)

    def begin(piece):
        @pl.when(chain == 0)
        def _():
            zbuf[piece, z] = base[piece]

        @pl.when(chain > 0)
        def _():
            remote(part_in.at[piece], part_in.at[piece], y_send.at[piece], y_recv.at[piece], (chain, me)).wait_recv()
            zbuf[piece, z] = base[piece] - jnp.sum(part_in[piece], axis=0)

        for offset in (4, 3, 5, 2, 6, 1, 7):
            peer = (z + offset) % SIDE
            remote(zbuf.at[piece, z], zbuf.at[piece, z], z_send.at[piece], z_recv.at[piece],
                   (chain, y * SIDE + peer)).start()

    def multiply(piece, hi, lo, target):
        both = stack[piece]
        wide_sum = jnp.dot(hi[...], both, preferred_element_type=F32)
        narrow = jnp.dot(lo[...], both[:, :LANES], preferred_element_type=F32)
        sums = wide_sum[:, :LANES] + wide_sum[:, LANES:] + narrow
        for row in range(SIDE):
            top = sums[row * own:row * own + fold_rows]
            bottom = sums[row * own + fold_rows:(row + 1) * own]
            target[piece, row] = jnp.where(left, top, bottom)

    def send_diag(piece):
        diag_in[piece, y] = diag_out[piece, y]
        for offset in (4, 3, 5, 2, 6, 1, 7):
            row = (y + offset) % SIDE
            remote(diag_out.at[piece, row], diag_in.at[piece, y], d_send.at[piece], d_recv.at[piece],
                   (chain, row * SIDE + z)).start()

    def finish(piece):
        seven = zbuf.at[piece, pl.ds(0, SIDE - 1)]
        remote(seven, seven, z_send.at[piece], z_recv.at[piece], (chain, me)).wait_recv()
        lane = iota((fold_rows, LANES), 1)
        imag = lane % (LANES // 2) >= LANES // 4
        for source in range(SIDE):
            block = zbuf[piece, source]
            turned = jnp.where(imag, pltpu.roll(block, LANES // 4, 1), -pltpu.roll(block, LANES - LANES // 4, 1))
            for part, value in enumerate((block, turned)):
                other = pltpu.roll(value, LANES // 2, 1)
                for side, wanted in enumerate((jnp.where(left, value, other), jnp.where(left, other, value))):
                    high, low = split(wanted)
                    at = part * span + source * own + side * fold_rows
                    stack[piece, at:at + fold_rows, :LANES] = high
                    stack[piece, at:at + fold_rows, LANES:] = low

        @pl.when(not_last)
        def _():
            multiply(piece, first_hi, first_lo, part_out)
            for row in range(SIDE):
                remote(part_out.at[piece, row], part_in.at[piece, y], y_send.at[piece], y_recv.at[piece],
                       (chain + 1, row * SIDE + z)).start()

        @pl.when(last)
        def _():
            multiply(piece, first_hi, first_lo, diag_out)
            send_diag(piece)

    def step(index, carry):
        @pl.when(index < pieces)
        def _():
            begin(index)

        @pl.when(index > 0)
        def _():
            finish(index - 1)

        return carry

    lax.fori_loop(0, pieces + 1, step, 0)

    @pl.when(not_last)
    def _():
        take_matrix(diag, second, 1, second_hi, second_lo)

        def solve(piece, carry):
            multiply(piece, second_hi, second_lo, diag_out)
            send_diag(piece)
            return carry

        lax.fori_loop(0, pieces, solve, 0)

    def collect(piece, carry):
        seven = diag_in.at[piece, pl.ds(0, SIDE - 1)]
        remote(seven, seven, d_send.at[piece], d_recv.at[piece], (chain, me)).wait_recv()
        out[piece] = jnp.sum(diag_in[piece], axis=0)
        return carry

    lax.fori_loop(0, pieces, collect, 0)

    remote(most, most, slot_send, slot_recv, (chain, me)).wait_send()
    seven = first.at[pl.ds(0, SIDE - 1)]
    remote(seven, seven, mat_send.at[0], mat_recv.at[0], (chain, me)).wait_send()

    @pl.when(not_last)
    def _():
        seven = second.at[pl.ds(0, SIDE - 1)]
        remote(seven, seven, mat_send.at[1], mat_recv.at[1], (chain, me)).wait_send()

    def drain(piece, carry):
        seven = zbuf.at[piece, pl.ds(0, SIDE - 1)]
        remote(seven, seven, z_send.at[piece], z_recv.at[piece], (chain, me)).wait_send()
        seven = diag_out.at[piece, pl.ds(0, SIDE - 1)]
        remote(seven, seven, d_send.at[piece], d_recv.at[piece], (chain, me)).wait_send()

        @pl.when(not_last)
        def _():
            remote(part_out.at[piece], part_out.at[piece], y_send.at[piece], y_recv.at[piece], (chain, me)).wait_send()

        return carry

    lax.fori_loop(0, pieces, drain, 0)


def body(chains, right_side, diag_inverse, coupling, updates, update_rows, tile_counts):
    pieces, halves, sources, own = right_side.shape
    fold_rows = own // 2
    group = SIDE * SIDE
    span = SIDE * own
    count_rows = updates.shape[0]
    folded = right_side.reshape(pieces, halves, sources, 2, fold_rows).transpose(0, 4, 3, 1, 2)
    folded = folded.reshape(pieces, fold_rows, LANES)
    vmem = pl.BlockSpec(memory_space=pltpu.VMEM)
    hbm = pl.BlockSpec(memory_space=pl.ANY)
    block = (pieces, SIDE, fold_rows, LANES)
    dma = pltpu.SemaphoreType.DMA
    solved = pl.pallas_call(
        functools.partial(kernel, chains),
        out_shape=jax.ShapeDtypeStruct(folded.shape, F32),
        in_specs=[vmem, vmem, vmem, pl.BlockSpec(memory_space=pltpu.SMEM), hbm, hbm],
        out_specs=vmem,
        scratch_shapes=[
            pltpu.VMEM((count_rows, 2 * LANES), F32),
            pltpu.VMEM((group, SLOTS, 2 * LANES), F32),
            pltpu.VMEM((group, SLOTS, 2 * LANES), F32),
            pltpu.VMEM((SIDE, 2, own, span), F32),
            pltpu.VMEM((SIDE, 2, own, span), F32),
            pltpu.VMEM((span, 2 * span), BF16),
            pltpu.VMEM((span, 2 * span), BF16),
            pltpu.VMEM((span, 2 * span), BF16),
            pltpu.VMEM((span, 2 * span), BF16),
            pltpu.VMEM((pieces, fold_rows, LANES), F32),
            pltpu.VMEM(block, F32),
            pltpu.VMEM(block, F32),
            pltpu.VMEM(block, F32),
            pltpu.VMEM(block, F32),
            pltpu.VMEM(block, F32),
            pltpu.VMEM((pieces, 2 * span, 2 * LANES), BF16),
            dma((2,)),
            dma,
            dma,
            dma((2,)),
            dma((2,)),
            dma((pieces,)),
            dma((pieces,)),
            dma((pieces,)),
            dma((pieces,)),
            dma((pieces,)),
            dma((pieces,)),
        ],
        compiler_params=pltpu.CompilerParams(collective_id=0, has_side_effects=True, vmem_limit_bytes=48 << 20),
    )(folded, updates, update_rows.reshape(1, count_rows), tile_counts, diag_inverse, coupling)
    solved = solved.reshape(pieces, fold_rows, 2, halves, sources).transpose(0, 3, 4, 2, 1)
    return solved.reshape(right_side.shape)


def solution(mesh):
    in_specs = (
        P(None, None, None, ("chain", "tile")),
        P(None, ("chain", "tile"), None),
        P(None, ("chain", "tile"), None),
        P(("chain", "tile"), None),
        P(("chain", "tile")),
        P(("chain", "tile")),
    )
    out_specs = P(None, None, None, ("chain", "tile"))
    run = functools.partial(body, mesh.shape["chain"])
    return jax.shard_map(run, mesh=mesh, in_specs=in_specs, out_specs=out_specs, check_vma=False)
```

```python
import functools

import jax
import jax.numpy as jnp
from jax import lax
from jax.experimental import pallas as pl
from jax.experimental.pallas import tpu as pltpu
from jax.sharding import PartitionSpec as P

MESH = pl.DeviceIdType.MESH
F32 = jnp.float32
BF16 = jnp.bfloat16
SIDE = 8
FOLD = 4
SLOTS = 8
LANES = 128


def remote(src, dst, send_sem, recv_sem, device):
    return pltpu.make_async_remote_copy(
        src_ref=src, dst_ref=dst, send_sem=send_sem, recv_sem=recv_sem, device_id=device, device_id_type=MESH
    )


def split(value):
    high = value.astype(BF16)
    return high, (value - high.astype(F32)).astype(BF16)


def iota(shape, axis):
    return lax.broadcasted_iota(jnp.int32, shape, axis)


def kernel(chains, rhs, upd, rows, counts, diag, coup, out, wide, slots_out, slots_in, raw, sorted_first, sorted_second, first, second,
           first_hi, first_lo, second_hi, second_lo, rhs_wide, base, zbuf, part_in, part_out, diag_in, diag_out, stack,
           local_sem, slot_send, slot_recv, mat_send, mat_recv, z_send, z_recv, y_send, y_recv, d_send, d_recv, core_done):
    pieces, fold_rows = base.shape[0], base.shape[1]
    own = rhs.shape[1]
    fold = own // fold_rows
    width = LANES // fold
    lane_group = lax.div(iota((fold_rows, LANES), 1), width)
    group = SIDE * SIDE
    span = SIDE * own
    chain = lax.axis_index("chain")
    me = lax.axis_index("tile")
    y, z = me // SIDE, me % SIDE
    not_last = chain < chains - 1
    last = chain == chains - 1
    odd = chain % 2
    across, along = y * odd + z * (1 - odd), z * odd + y * (1 - odd)
    across_step, along_step = 1 + (SIDE - 1) * odd, SIDE - (SIDE - 1) * odd

    def place_of(across_at, along_at):
        return across_at * across_step + along_at * along_step

    def folded(parts):
        result = parts[fold - 1]
        for index in range(fold - 1):
            result = jnp.where(lane_group == index, parts[index], result)
        return result

    def spread(value):
        turns = [value] + [pltpu.roll(value, index * width, 1) for index in range(1, fold)]
        result = []
        for index in range(fold):
            wanted = turns[(fold - 1 - index) % fold]
            for at in range(fold - 1):
                wanted = jnp.where(lane_group == at, turns[(at - index) % fold], wanted)
            result.append(wanted)
        return result

    barrier = pltpu.get_barrier_semaphore()

    def greet(offset, carry):
        pl.semaphore_signal(barrier, inc=1, device_id=(chain, (me + offset) % group), device_id_type=MESH)
        return carry

    lax.fori_loop(1, group, greet, 0)

    @pl.when(not_last)
    def _():
        for row in range(SIDE):
            pl.semaphore_signal(barrier, inc=1, device_id=(chain + 1, place_of(across, row)), device_id_type=MESH)

    @pl.when(chain > 0)
    def _():
        for row in range(SIDE):
            pl.semaphore_signal(barrier, inc=1, device_id=(chain - 1, place_of(row, along)), device_id_type=MESH)

    def load(source, which):
        pltpu.make_async_copy(source, raw, local_sem.at[which]).start()

    def order(ordered, which):
        pltpu.make_async_copy(raw, raw, local_sem.at[which]).wait()
        near = iota((own, LANES), 1) < LANES // 2

        def pair(index, carry):
            for part in range(2):
                for group_at in range(SIDE // 2):
                    begin_at = [pl.multiple_of((2 * group_at + k) * span + index * LANES, LANES) for k in range(2)]
                    one, two = [raw[part, :, pl.ds(at, LANES)] for at in begin_at]
                    lanes = slice(group_at * LANES, (group_at + 1) * LANES)
                    ordered[2 * index, part, :, lanes] = jnp.where(near, one, pltpu.roll(two, LANES // 2, 1))
                    ordered[2 * index + 1, part, :, lanes] = jnp.where(near, pltpu.roll(one, LANES // 2, 1), two)
            return carry

        lax.fori_loop(0, SIDE // 2, pair, 0)

    @pl.when((odd == 1) & not_last)
    def _():
        load(coup, 0)

    @pl.when(last)
    def _():
        load(diag, 0)

    columns, count_rows = upd.shape
    some = width // 2
    wide[columns:] = jnp.zeros_like(wide[columns:])
    rhs_wide[columns:] = jnp.zeros_like(rhs_wide[columns:])
    per_batch = LANES // (2 * width)
    for piece in range(pieces):
        for part in range(2):
            source = (piece // per_batch) * (LANES // 2) + part * (LANES // 4) + (piece % per_batch) * some
            target = piece * width + part * some
            wide[target:target + some] = upd[source:source + some]
            rhs_wide[target:target + some] = rhs[source:source + some]
    row_of = rows[...]
    owner = lax.div(row_of, own)
    local = (row_of - owner * own).astype(F32)
    lane = iota((1, count_rows), 1)
    half = count_rows // 2
    live = jnp.where(lane < half, lane, lane - half) < jnp.where(lane < half, counts[0], counts[1])
    hits = (iota((group, count_rows), 0) == owner).astype(F32)
    before = (iota((count_rows, count_rows), 0) < iota((count_rows, count_rows), 1)).astype(F32).astype(BF16)
    earlier = jnp.dot(hits.astype(BF16), before, preferred_element_type=F32)
    rank = jnp.sum(hits * earlier, axis=0, keepdims=True)
    slot = jnp.where(live, owner.astype(F32) * SLOTS + rank, -1.0)
    pick = iota((group * SLOTS, count_rows), 0).astype(F32) == slot
    place = jnp.sum(jnp.where(pick, local, 0.0), axis=1, keepdims=True)
    pick = pick.astype(F32).astype(BF16)
    by_columns = (((1,), (1,)), ((), ()))
    payload = 0.0
    for part in split(wide[...]):
        payload += lax.dot_general(pick, part, by_columns, preferred_element_type=F32)
    payload = jnp.where(iota(payload.shape, 1) == columns, place, payload)
    slots_out[...] = payload.reshape(slots_out.shape)

    same = (iota((own, own), 0) == iota((own, own), 1)).astype(F32).astype(BF16)
    high, low = split(rhs_wide[...])
    rest = (rhs_wide[...] - high.astype(F32) - low.astype(F32)).astype(BF16)
    rhs_rows = 0.0
    for part in (rest, low, high):
        rhs_rows += lax.dot_general(same, part, by_columns, preferred_element_type=F32)

    @pl.when(odd == 1)
    def _():
        order(sorted_first, 0)

    ends = (chain == 0) | last

    @pl.when(ends)
    def _():
        pl.semaphore_wait(barrier, group - 1 + SIDE)

    @pl.when(jnp.logical_not(ends))
    def _():
        pl.semaphore_wait(barrier, group - 1 + 2 * SIDE)

    def send_slots(offset, carry):
        peer = (me + offset) % group
        remote(slots_out.at[peer], slots_in.at[me], slot_send, slot_recv, (chain, peer)).start()
        return carry

    def columns_of(source, row):
        return source.at[:, :, pl.ds(pl.multiple_of(row * span, span), span)]

    def send_even(source, target, which):
        pltpu.make_async_copy(columns_of(source, along), target.at[along], local_sem.at[which]).start()
        for offset in (4, 3, 5, 2, 6, 1, 7):
            row = (along + offset) % SIDE
            remote(columns_of(source, row), target.at[along], mat_send.at[which], mat_recv.at[which],
                   (chain, place_of(across, row))).start()

    def send_odd(ordered, target, which):
        pltpu.make_async_copy(ordered.at[along], target.at[along], local_sem.at[which]).start()
        for offset in (4, 3, 5, 2, 6, 1, 7):
            row = (along + offset) % SIDE
            remote(ordered.at[row], target.at[along], mat_send.at[which], mat_recv.at[which],
                   (chain, place_of(across, row))).start()

    def take_matrix(target, which, hi, lo):
        pltpu.make_async_copy(target.at[along], target.at[along], local_sem.at[which]).wait()
        seven = target.at[pl.ds(0, SIDE - 1)]
        remote(seven, seven, mat_send.at[which], mat_recv.at[which], (chain, me)).wait_recv()

        def cut(row, carry):
            for part in range(2):
                high, low = split(target[row, part])
                at = pl.ds(pl.multiple_of(row * own, own), own)
                hi[at, part * span:(part + 1) * span] = high
                lo[at, part * span:(part + 1) * span] = low
            return carry

        lax.fori_loop(0, SIDE, cut, 0)

    slots_in[me] = slots_out[me]

    @pl.when(odd == 0)
    def _():
        lax.fori_loop(1, group, send_slots, 0)
        send_even(coup, first, 0)

    @pl.when(odd == 1)
    def _():
        send_odd(sorted_first, first, 0)
        take_matrix(first, 0, first_hi, first_lo)
        lax.fori_loop(1, group, send_slots, 0)

    most = slots_in.at[pl.ds(0, group - 1)]
    remote(most, most, slot_send, slot_recv, (chain, me)).wait_recv()
    arrived = slots_in[...].reshape(group * SLOTS, slots_in.shape[2])
    pick = (arrived[:, columns:columns + 1] == iota((group * SLOTS, own), 1).astype(F32)).astype(F32).astype(BF16)
    high, low = split(arrived)
    by_rows = (((0,), (0,)), ((), ()))
    total = (lax.dot_general(pick, high, by_rows, preferred_element_type=F32)
             + lax.dot_general(pick, low, by_rows, preferred_element_type=F32))
    total = rhs_rows - total
    for piece in range(pieces):
        column = piece * width
        tile = total[:, column // LANES * LANES:column // LANES * LANES + LANES]
        parts = []
        for index in range(fold):
            turn = (index * width - column) % LANES
            part = tile[index * fold_rows:(index + 1) * fold_rows]
            parts.append(pltpu.roll(part, turn, 1) if turn else part)
        base[piece] = folded(parts)

    @pl.when(odd == 0)
    def _():
        take_matrix(first, 0, first_hi, first_lo)

    def send_second():
        @pl.when(odd == 0)
        def _():
            send_even(diag, second, 1)

        @pl.when((odd == 1) & not_last)
        def _():
            load(diag, 1)
            order(sorted_second, 1)
            send_odd(sorted_second, second, 1)

    late = chain < chains // 2

    @pl.when(jnp.logical_not(late))
    def _():
        send_second()

    def begin(piece):
        @pl.when(chain == 0)
        def _():
            zbuf[piece, across] = base[piece]

        @pl.when(chain > 0)
        def _():
            remote(part_in.at[piece], part_in.at[piece], y_send.at[piece], y_recv.at[piece], (chain, me)).wait_recv()
            zbuf[piece, across] = base[piece] - jnp.sum(part_in[piece], axis=0)

        for offset in (4, 3, 5, 2, 6, 1, 7):
            peer = (across + offset) % SIDE
            remote(zbuf.at[piece, across], zbuf.at[piece, across], z_send.at[piece], z_recv.at[piece],
                   (chain, place_of(peer, along))).start()

    def multiply(piece, hi, lo, target):
        both = stack[piece]
        wide_sum = jnp.dot(hi[...], both, preferred_element_type=F32)
        narrow = jnp.dot(lo[...], both[:, :LANES], preferred_element_type=F32)
        sums = wide_sum[:, :LANES] + wide_sum[:, LANES:] + narrow
        for row in range(SIDE):
            target[piece, row] = folded(
                [sums[row * own + at * fold_rows:row * own + (at + 1) * fold_rows] for at in range(fold)])

    def send_diag(piece):
        diag_in[piece, along] = diag_out[piece, along]
        for offset in (4, 3, 5, 2, 6, 1, 7):
            row = (along + offset) % SIDE
            remote(diag_out.at[piece, row], diag_in.at[piece, along], d_send.at[piece], d_recv.at[piece],
                   (chain, place_of(across, row))).start()

    def finish(piece):
        seven = zbuf.at[piece, pl.ds(0, SIDE - 1)]
        remote(seven, seven, z_send.at[piece], z_recv.at[piece], (chain, me)).wait_recv()
        lane = iota((fold_rows, LANES), 1)
        imag = lane % width >= some
        for source in range(SIDE):
            block = zbuf[piece, source]
            turned = jnp.where(imag, pltpu.roll(block, some, 1), -pltpu.roll(block, LANES - some, 1))
            for part, value in enumerate((block, turned)):
                for index, wanted in enumerate(spread(value)):
                    high, low = split(wanted)
                    at = part * span + source * own + index * fold_rows
                    stack[piece, at:at + fold_rows, :LANES] = high
                    stack[piece, at:at + fold_rows, LANES:] = low

        @pl.when(not_last)
        def _():
            multiply(piece, first_hi, first_lo, part_out)
            for row in range(SIDE):
                remote(part_out.at[piece, row], part_in.at[piece, along], y_send.at[piece], y_recv.at[piece],
                       (chain + 1, place_of(across, row))).start()

        @pl.when(last)
        def _():
            multiply(piece, first_hi, first_lo, diag_out)
            send_diag(piece)

    def step(index, carry):
        @pl.when(index < pieces)
        def _():
            begin(index)

        @pl.when(index > 0)
        def _():
            finish(index - 1)

        return carry

    lax.fori_loop(0, pieces + 1, step, 0)

    @pl.when(late & (odd == 1))
    def _():
        pl.semaphore_signal(core_done, inc=1, device_id=(chain - 1, me), device_id_type=MESH)
        send_second()

    @pl.when(late & (odd == 0))
    def _():
        pl.semaphore_wait(core_done, 1)
        send_second()

    @pl.when(not_last)
    def _():
        take_matrix(second, 1, second_hi, second_lo)

        def solve(piece, carry):
            multiply(piece, second_hi, second_lo, diag_out)
            send_diag(piece)
            return carry

        lax.fori_loop(0, pieces, solve, 0)

    def collect(piece, carry):
        seven = diag_in.at[piece, pl.ds(0, SIDE - 1)]
        remote(seven, seven, d_send.at[piece], d_recv.at[piece], (chain, me)).wait_recv()
        out[piece] = jnp.sum(diag_in[piece], axis=0)
        return carry

    lax.fori_loop(0, pieces, collect, 0)

    remote(most, most, slot_send, slot_recv, (chain, me)).wait_send()
    seven = first.at[pl.ds(0, SIDE - 1)]
    remote(seven, seven, mat_send.at[0], mat_recv.at[0], (chain, me)).wait_send()

    @pl.when(not_last)
    def _():
        seven = second.at[pl.ds(0, SIDE - 1)]
        remote(seven, seven, mat_send.at[1], mat_recv.at[1], (chain, me)).wait_send()

    def drain(piece, carry):
        seven = zbuf.at[piece, pl.ds(0, SIDE - 1)]
        remote(seven, seven, z_send.at[piece], z_recv.at[piece], (chain, me)).wait_send()
        seven = diag_out.at[piece, pl.ds(0, SIDE - 1)]
        remote(seven, seven, d_send.at[piece], d_recv.at[piece], (chain, me)).wait_send()

        @pl.when(not_last)
        def _():
            remote(part_out.at[piece], part_out.at[piece], y_send.at[piece], y_recv.at[piece], (chain, me)).wait_send()

        return carry

    lax.fori_loop(0, pieces, drain, 0)


def body(chains, right_side, diag_inverse, coupling, updates, update_rows, tile_counts):
    batches, halves, sources, own = right_side.shape
    fold = FOLD
    fold_rows, width = own // fold, LANES // fold
    pieces = batches * halves * sources // width
    group = SIDE * SIDE
    span = SIDE * own
    count_rows = updates.shape[0]
    vmem = pl.BlockSpec(memory_space=pltpu.VMEM)
    hbm = pl.BlockSpec(memory_space=pltpu.HBM)
    block = (pieces, SIDE, fold_rows, LANES)
    dma = pltpu.SemaphoreType.DMA
    solved = pl.pallas_call(
        functools.partial(kernel, chains),
        out_shape=jax.ShapeDtypeStruct((pieces, fold_rows, LANES), F32),
        in_specs=[vmem, vmem, vmem, pl.BlockSpec(memory_space=pltpu.SMEM), hbm, hbm],
        out_specs=vmem,
        scratch_shapes=[
            pltpu.VMEM((2 * LANES, count_rows), F32),
            pltpu.VMEM((group, SLOTS, 2 * LANES), F32),
            pltpu.VMEM((group, SLOTS, 2 * LANES), F32),
            pltpu.VMEM((2, own, group * own), F32),
            pltpu.VMEM((SIDE, 2, own, span), F32),
            pltpu.VMEM((SIDE, 2, own, span), F32),
            pltpu.VMEM((SIDE, 2, own, span), F32),
            pltpu.VMEM((SIDE, 2, own, span), F32),
            pltpu.VMEM((span, 2 * span), BF16),
            pltpu.VMEM((span, 2 * span), BF16),
            pltpu.VMEM((span, 2 * span), BF16),
            pltpu.VMEM((span, 2 * span), BF16),
            pltpu.VMEM((2 * LANES, own), F32),
            pltpu.VMEM((pieces, fold_rows, LANES), F32),
            pltpu.VMEM(block, F32),
            pltpu.VMEM(block, F32),
            pltpu.VMEM(block, F32),
            pltpu.VMEM(block, F32),
            pltpu.VMEM(block, F32),
            pltpu.VMEM((pieces, 2 * span, 2 * LANES), BF16),
            dma((2,)),
            dma,
            dma,
            dma((2,)),
            dma((2,)),
            dma((pieces,)),
            dma((pieces,)),
            dma((pieces,)),
            dma((pieces,)),
            dma((pieces,)),
            dma((pieces,)),
            pltpu.SemaphoreType.REGULAR,
        ],
        compiler_params=pltpu.CompilerParams(collective_id=0, has_side_effects=True, vmem_limit_bytes=63 << 20),
    )(right_side.reshape(batches * halves * sources, own), updates.T, update_rows.reshape(1, count_rows), tile_counts, diag_inverse, coupling)
    solved = solved.reshape(batches, pieces // batches, fold_rows, fold, halves, width // halves)
    return solved.transpose(0, 4, 1, 5, 3, 2).reshape(right_side.shape)


def solution(mesh):
    in_specs = (
        P(None, None, None, ("chain", "tile")),
        P(None, ("chain", "tile"), None),
        P(None, ("chain", "tile"), None),
        P(("chain", "tile"), None),
        P(("chain", "tile")),
        P(("chain", "tile")),
    )
    out_specs = P(None, None, None, ("chain", "tile"))
    run = functools.partial(body, mesh.shape["chain"])
    return jax.shard_map(run, mesh=mesh, in_specs=in_specs, out_specs=out_specs, check_vma=False)
```

```python
import functools

import jax
import jax.numpy as jnp
from jax import lax
from jax.experimental import pallas as pl
from jax.experimental.pallas import tpu as pltpu
from jax.sharding import PartitionSpec as P

MESH = pl.DeviceIdType.MESH
F32 = jnp.float32
BF16 = jnp.bfloat16
SIDE = 8
FOLD = 4
SLOTS = 8
LANES = 128


def remote(src, dst, send_sem, recv_sem, device):
    return pltpu.make_async_remote_copy(
        src_ref=src, dst_ref=dst, send_sem=send_sem, recv_sem=recv_sem, device_id=device, device_id_type=MESH
    )


def split(value):
    high = value.astype(BF16)
    return high, (value - high.astype(F32)).astype(BF16)


def iota(shape, axis):
    return lax.broadcasted_iota(jnp.int32, shape, axis)


def kernel(chains, rhs, upd, rows, counts, diag, coup, out, wide, slots_out, slots_in, raw, sorted_first, sorted_second, first, second,
           first_hi, first_lo, second_hi, second_lo, rhs_wide, base, zbuf, part_in, part_out, diag_in, diag_out, stack,
           local_sem, slot_send, slot_recv, mat_send, mat_recv, z_send, z_recv, y_send, y_recv, d_send, d_recv, core_done):
    pieces, fold_rows = base.shape[0], base.shape[1]
    own = rhs.shape[1]
    fold = own // fold_rows
    width = LANES // fold
    lane_group = lax.div(iota((fold_rows, LANES), 1), width)
    group = SIDE * SIDE
    span = SIDE * own
    chain = lax.axis_index("chain")
    me = lax.axis_index("tile")
    y, z = me // SIDE, me % SIDE
    not_last = chain < chains - 1
    last = chain == chains - 1
    odd = chain % 2
    across, along = y * odd + z * (1 - odd), z * odd + y * (1 - odd)
    across_step, along_step = 1 + (SIDE - 1) * odd, SIDE - (SIDE - 1) * odd

    def place_of(across_at, along_at):
        return across_at * across_step + along_at * along_step

    def folded(parts):
        result = parts[fold - 1]
        for index in range(fold - 1):
            result = jnp.where(lane_group == index, parts[index], result)
        return result

    def spread(value):
        turns = [value] + [pltpu.roll(value, index * width, 1) for index in range(1, fold)]
        result = []
        for index in range(fold):
            wanted = turns[(fold - 1 - index) % fold]
            for at in range(fold - 1):
                wanted = jnp.where(lane_group == at, turns[(at - index) % fold], wanted)
            result.append(wanted)
        return result

    barrier = pltpu.get_barrier_semaphore()

    def greet(offset, carry):
        pl.semaphore_signal(barrier, inc=1, device_id=(chain, (me + offset) % group), device_id_type=MESH)
        return carry

    lax.fori_loop(1, group, greet, 0)

    @pl.when(not_last)
    def _():
        for row in range(SIDE):
            pl.semaphore_signal(barrier, inc=1, device_id=(chain + 1, place_of(across, row)), device_id_type=MESH)

    @pl.when(chain > 0)
    def _():
        for row in range(SIDE):
            pl.semaphore_signal(barrier, inc=1, device_id=(chain - 1, place_of(row, along)), device_id_type=MESH)

    def load(source, which):
        pltpu.make_async_copy(source, raw, local_sem.at[which]).start()

    def order(ordered, which):
        pltpu.make_async_copy(raw, raw, local_sem.at[which]).wait()
        near = iota((own, LANES), 1) < LANES // 2

        def pair(index, carry):
            for part in range(2):
                for group_at in range(SIDE // 2):
                    begin_at = [pl.multiple_of((2 * group_at + k) * span + index * LANES, LANES) for k in range(2)]
                    one, two = [raw[part, :, pl.ds(at, LANES)] for at in begin_at]
                    lanes = slice(group_at * LANES, (group_at + 1) * LANES)
                    ordered[2 * index, part, :, lanes] = jnp.where(near, one, pltpu.roll(two, LANES // 2, 1))
                    ordered[2 * index + 1, part, :, lanes] = jnp.where(near, pltpu.roll(one, LANES // 2, 1), two)
            return carry

        lax.fori_loop(0, SIDE // 2, pair, 0)

    @pl.when((odd == 1) & not_last)
    def _():
        load(coup, 0)

    @pl.when(last)
    def _():
        load(diag, 0)

    columns, count_rows = upd.shape
    some = width // 2
    wide[columns:] = jnp.zeros_like(wide[columns:])
    rhs_wide[columns:] = jnp.zeros_like(rhs_wide[columns:])
    per_batch = LANES // (2 * width)
    for piece in range(pieces):
        for part in range(2):
            source = (piece // per_batch) * (LANES // 2) + part * (LANES // 4) + (piece % per_batch) * some
            target = piece * width + part * some
            wide[target:target + some] = upd[source:source + some]
            rhs_wide[target:target + some] = rhs[source:source + some]
    row_of = rows[...]
    owner = lax.div(row_of, own)
    local = (row_of - owner * own).astype(F32)
    lane = iota((1, count_rows), 1)
    half = count_rows // 2
    live = jnp.where(lane < half, lane, lane - half) < jnp.where(lane < half, counts[0], counts[1])
    hits = (iota((group, count_rows), 0) == owner).astype(F32)
    before = (iota((count_rows, count_rows), 0) < iota((count_rows, count_rows), 1)).astype(F32).astype(BF16)
    earlier = jnp.dot(hits.astype(BF16), before, preferred_element_type=F32)
    rank = jnp.sum(hits * earlier, axis=0, keepdims=True)
    slot = jnp.where(live, owner.astype(F32) * SLOTS + rank, -1.0)
    pick = iota((group * SLOTS, count_rows), 0).astype(F32) == slot
    place = jnp.sum(jnp.where(pick, local, 0.0), axis=1, keepdims=True)
    pick = pick.astype(F32).astype(BF16)
    by_columns = (((1,), (1,)), ((), ()))
    payload = 0.0
    for part in split(wide[...]):
        payload += lax.dot_general(pick, part, by_columns, preferred_element_type=F32)
    payload = jnp.where(iota(payload.shape, 1) == columns, place, payload)
    slots_out[...] = payload.reshape(slots_out.shape)

    same = (iota((own, own), 0) == iota((own, own), 1)).astype(F32).astype(BF16)
    high, low = split(rhs_wide[...])
    rest = (rhs_wide[...] - high.astype(F32) - low.astype(F32)).astype(BF16)
    rhs_rows = 0.0
    for part in (rest, low, high):
        rhs_rows += lax.dot_general(same, part, by_columns, preferred_element_type=F32)

    @pl.when(odd == 1)
    def _():
        order(sorted_first, 0)

    ends = (chain == 0) | last

    @pl.when(ends)
    def _():
        pl.semaphore_wait(barrier, group - 1 + SIDE)

    @pl.when(jnp.logical_not(ends))
    def _():
        pl.semaphore_wait(barrier, group - 1 + 2 * SIDE)

    def send_slots(offset, carry):
        peer = (me + offset) % group
        remote(slots_out.at[peer], slots_in.at[me], slot_send, slot_recv, (chain, peer)).start()
        return carry

    def columns_of(source, row):
        return source.at[:, :, pl.ds(pl.multiple_of(row * span, span), span)]

    def send_even(source, target, which):
        pltpu.make_async_copy(columns_of(source, along), target.at[along], local_sem.at[which]).start()
        for offset in (4, 3, 5, 2, 6, 1, 7):
            row = (along + offset) % SIDE
            remote(columns_of(source, row), target.at[along], mat_send.at[which], mat_recv.at[which],
                   (chain, place_of(across, row))).start()

    def send_odd(ordered, target, which):
        pltpu.make_async_copy(ordered.at[along], target.at[along], local_sem.at[which]).start()
        for offset in (4, 3, 5, 2, 6, 1, 7):
            row = (along + offset) % SIDE
            remote(ordered.at[row], target.at[along], mat_send.at[which], mat_recv.at[which],
                   (chain, place_of(across, row))).start()

    def take_matrix(target, which, hi, lo):
        pltpu.make_async_copy(target.at[along], target.at[along], local_sem.at[which]).wait()
        seven = target.at[pl.ds(0, SIDE - 1)]
        remote(seven, seven, mat_send.at[which], mat_recv.at[which], (chain, me)).wait_recv()

        shift = (SIDE + 2 - across) % SIDE * own
        half_span = span // 2

        def cut(row, carry):
            for part in range(2):
                high, low = split(pltpu.roll(target[row, part], shift, 1))
                at = pl.ds(pl.multiple_of(row * own, own), own)
                for side in range(2):
                    here = side * span + part * half_span
                    hi[at, here:here + half_span] = high[:, side * half_span:(side + 1) * half_span]
                    lo[at, here:here + half_span] = low[:, side * half_span:(side + 1) * half_span]
            return carry

        lax.fori_loop(0, SIDE, cut, 0)

    lax.fori_loop(1, group, send_slots, 0)
    slots_in[me] = slots_out[me]

    @pl.when(odd == 0)
    def _():
        send_even(coup, first, 0)

    @pl.when(odd == 1)
    def _():
        send_odd(sorted_first, first, 0)

    most = slots_in.at[pl.ds(0, group - 1)]
    remote(most, most, slot_send, slot_recv, (chain, me)).wait_recv()
    arrived = slots_in[...].reshape(group * SLOTS, slots_in.shape[2])
    pick = (arrived[:, columns:columns + 1] == iota((group * SLOTS, own), 1).astype(F32)).astype(F32).astype(BF16)
    high, low = split(arrived)
    by_rows = (((0,), (0,)), ((), ()))
    total = (lax.dot_general(pick, high, by_rows, preferred_element_type=F32)
             + lax.dot_general(pick, low, by_rows, preferred_element_type=F32))
    total = rhs_rows - total
    for piece in range(pieces):
        column = piece * width
        tile = total[:, column // LANES * LANES:column // LANES * LANES + LANES]
        parts = []
        for index in range(fold):
            turn = (index * width - column) % LANES
            part = tile[index * fold_rows:(index + 1) * fold_rows]
            parts.append(pltpu.roll(part, turn, 1) if turn else part)
        base[piece] = folded(parts)

    def send_second():
        @pl.when(odd == 0)
        def _():
            send_even(diag, second, 1)

        @pl.when((odd == 1) & not_last)
        def _():
            load(diag, 1)
            order(sorted_second, 1)
            send_odd(sorted_second, second, 1)

    def begin(piece):
        @pl.when(chain == 0)
        def _():
            zbuf[piece, across] = base[piece]

        @pl.when(chain > 0)
        def _():
            remote(part_in.at[piece], part_in.at[piece], y_send.at[piece], y_recv.at[piece], (chain, me)).wait_recv()
            zbuf[piece, across] = base[piece] - jnp.sum(part_in[piece], axis=0)

        for offset in (4, 3, 5, 2, 6, 1, 7):
            peer = (across + offset) % SIDE
            side = 0 if offset in (1, 2, 7) else 1
            remote(zbuf.at[piece, across], zbuf.at[piece, across], z_send.at[piece], z_recv.at[piece, side],
                   (chain, place_of(peer, along))).start()

    @pl.when(chain == 0)
    def _():
        def start(piece, carry):
            begin(piece)
            return carry

        lax.fori_loop(0, pieces, start, 0)

    take_matrix(first, 0, first_hi, first_lo)

    late = chain < chains // 2

    @pl.when(jnp.logical_not(late))
    def _():
        send_second()

    def product(hi, lo, both):
        wide_sum = jnp.dot(hi, both, preferred_element_type=F32)
        narrow = jnp.dot(lo, both[:, :LANES], preferred_element_type=F32)
        return wide_sum[:, :LANES] + wide_sum[:, LANES:] + narrow

    def store(piece, sums, target):
        for row in range(SIDE):
            target[piece, row] = folded(
                [sums[row * own + at * fold_rows:row * own + (at + 1) * fold_rows] for at in range(fold)])

    def send_diag(piece, source):
        diag_in[piece, along] = source[piece, along]
        for offset in (4, 3, 5, 2, 6, 1, 7):
            row = (along + offset) % SIDE
            remote(source.at[piece, row], diag_in.at[piece, along], d_send.at[piece], d_recv.at[piece],
                   (chain, place_of(across, row))).start()

    def finish(piece):
        lane = iota((fold_rows, LANES), 1)
        imag = lane % width >= some
        sums = 0.0
        for side in range(2):
            some_blocks = zbuf.at[piece, pl.ds(0, 3 + side)]
            remote(some_blocks, some_blocks, z_send.at[piece], z_recv.at[piece, side], (chain, me)).wait_recv()
            for near in range(SIDE // 2):
                block = zbuf[piece, (across + side * (SIDE // 2) + near + SIDE - 2) % SIDE]
                turned = jnp.where(imag, pltpu.roll(block, some, 1), -pltpu.roll(block, LANES - some, 1))
                for part, value in enumerate((block, turned)):
                    for index, wanted in enumerate(spread(value)):
                        high, low = split(wanted)
                        at = side * span + part * (span // 2) + near * own + index * fold_rows
                        stack[piece, at:at + fold_rows, :LANES] = high
                        stack[piece, at:at + fold_rows, LANES:] = low
            at = slice(side * span, (side + 1) * span)
            sums = sums + product(first_hi[:, at], first_lo[:, at], stack[piece, at])
        store(piece, sums, part_out)

        @pl.when(not_last)
        def _():
            for offset in (4, 3, 5, 2, 6, 1, 7, 0):
                row = (along + offset) % SIDE
                remote(part_out.at[piece, row], part_in.at[piece, along], y_send.at[piece], y_recv.at[piece],
                       (chain + 1, place_of(across, row))).start()

        @pl.when(last)
        def _():
            send_diag(piece, part_out)

    def step(index, carry):
        @pl.when((index < pieces) & (chain > 0))
        def _():
            begin(index)

        @pl.when(index > 0)
        def _():
            finish(index - 1)

        return carry

    lax.fori_loop(0, pieces + 1, step, 0)

    @pl.when(late & (odd == 1))
    def _():
        pl.semaphore_signal(core_done, inc=1, device_id=(chain - 1, me), device_id_type=MESH)
        send_second()

    @pl.when(late & (odd == 0))
    def _():
        pl.semaphore_wait(core_done, 1)
        send_second()

    @pl.when(not_last)
    def _():
        take_matrix(second, 1, second_hi, second_lo)

        def solve(piece, carry):
            store(piece, product(second_hi[...], second_lo[...], stack[piece]), diag_out)
            send_diag(piece, diag_out)
            return carry

        lax.fori_loop(0, pieces, solve, 0)

    def collect(piece, carry):
        seven = diag_in.at[piece, pl.ds(0, SIDE - 1)]
        remote(seven, seven, d_send.at[piece], d_recv.at[piece], (chain, me)).wait_recv()
        out[piece] = jnp.sum(diag_in[piece], axis=0)
        return carry

    lax.fori_loop(0, pieces, collect, 0)

    remote(most, most, slot_send, slot_recv, (chain, me)).wait_send()
    seven = first.at[pl.ds(0, SIDE - 1)]
    remote(seven, seven, mat_send.at[0], mat_recv.at[0], (chain, me)).wait_send()

    @pl.when(not_last)
    def _():
        seven = second.at[pl.ds(0, SIDE - 1)]
        remote(seven, seven, mat_send.at[1], mat_recv.at[1], (chain, me)).wait_send()

    def drain(piece, carry):
        seven = zbuf.at[piece, pl.ds(0, SIDE - 1)]
        remote(seven, seven, z_send.at[piece], z_recv.at[piece, 0], (chain, me)).wait_send()
        seven = diag_out.at[piece, pl.ds(0, SIDE - 1)]
        remote(seven, seven, d_send.at[piece], d_recv.at[piece], (chain, me)).wait_send()

        @pl.when(not_last)
        def _():
            remote(part_out.at[piece], part_out.at[piece], y_send.at[piece], y_recv.at[piece], (chain, me)).wait_send()

        return carry

    lax.fori_loop(0, pieces, drain, 0)


def body(chains, right_side, diag_inverse, coupling, updates, update_rows, tile_counts):
    batches, halves, sources, own = right_side.shape
    fold = FOLD
    fold_rows, width = own // fold, LANES // fold
    pieces = batches * halves * sources // width
    group = SIDE * SIDE
    span = SIDE * own
    count_rows = updates.shape[0]
    vmem = pl.BlockSpec(memory_space=pltpu.VMEM)
    hbm = pl.BlockSpec(memory_space=pltpu.HBM)
    block = (pieces, SIDE, fold_rows, LANES)
    dma = pltpu.SemaphoreType.DMA
    solved = pl.pallas_call(
        functools.partial(kernel, chains),
        out_shape=jax.ShapeDtypeStruct((pieces, fold_rows, LANES), F32),
        in_specs=[vmem, vmem, vmem, pl.BlockSpec(memory_space=pltpu.SMEM), hbm, hbm],
        out_specs=vmem,
        scratch_shapes=[
            pltpu.VMEM((2 * LANES, count_rows), F32),
            pltpu.VMEM((group, SLOTS, 2 * LANES), F32),
            pltpu.VMEM((group, SLOTS, 2 * LANES), F32),
            pltpu.VMEM((2, own, group * own), F32),
            pltpu.VMEM((SIDE, 2, own, span), F32),
            pltpu.VMEM((SIDE, 2, own, span), F32),
            pltpu.VMEM((SIDE, 2, own, span), F32),
            pltpu.VMEM((SIDE, 2, own, span), F32),
            pltpu.VMEM((span, 2 * span), BF16),
            pltpu.VMEM((span, 2 * span), BF16),
            pltpu.VMEM((span, 2 * span), BF16),
            pltpu.VMEM((span, 2 * span), BF16),
            pltpu.VMEM((2 * LANES, own), F32),
            pltpu.VMEM((pieces, fold_rows, LANES), F32),
            pltpu.VMEM(block, F32),
            pltpu.VMEM(block, F32),
            pltpu.VMEM(block, F32),
            pltpu.VMEM(block, F32),
            pltpu.VMEM(block, F32),
            pltpu.VMEM((pieces, 2 * span, 2 * LANES), BF16),
            dma((2,)),
            dma,
            dma,
            dma((2,)),
            dma((2,)),
            dma((pieces,)),
            dma((pieces, 2)),
            dma((pieces,)),
            dma((pieces,)),
            dma((pieces,)),
            dma((pieces,)),
            pltpu.SemaphoreType.REGULAR,
        ],
        compiler_params=pltpu.CompilerParams(collective_id=0, has_side_effects=True, vmem_limit_bytes=63 << 20),
    )(right_side.reshape(batches * halves * sources, own), updates.T, update_rows.reshape(1, count_rows), tile_counts, diag_inverse, coupling)
    solved = solved.reshape(batches, pieces // batches, fold_rows, fold, halves, width // halves)
    return solved.transpose(0, 4, 1, 5, 3, 2).reshape(right_side.shape)


def solution(mesh):
    in_specs = (
        P(None, None, None, ("chain", "tile")),
        P(None, ("chain", "tile"), None),
        P(None, ("chain", "tile"), None),
        P(("chain", "tile"), None),
        P(("chain", "tile")),
        P(("chain", "tile")),
    )
    out_specs = P(None, None, None, ("chain", "tile"))
    run = functools.partial(body, mesh.shape["chain"])
    return jax.shard_map(run, mesh=mesh, in_specs=in_specs, out_specs=out_specs, check_vma=False)
```

```python
import functools

import jax
import jax.numpy as jnp
from jax import lax
from jax.experimental import pallas as pl
from jax.experimental.pallas import tpu as pltpu
from jax.sharding import PartitionSpec as P

MESH = pl.DeviceIdType.MESH
F32 = jnp.float32
BF16 = jnp.bfloat16
SIDE = 8
FOLD = 4
AHEAD = 3
SLOTS = 8
LANES = 128


def remote(src, dst, send_sem, recv_sem, device):
    return pltpu.make_async_remote_copy(
        src_ref=src, dst_ref=dst, send_sem=send_sem, recv_sem=recv_sem, device_id=device, device_id_type=MESH
    )


def split(value):
    high = value.astype(BF16)
    return high, (value - high.astype(F32)).astype(BF16)


def iota(shape, axis):
    return lax.broadcasted_iota(jnp.int32, shape, axis)


def kernel(chains, rhs, upd, rows, counts, diag, coup, out, wide, slots_out, slots_in, raw, sorted_first, sorted_second, first, second,
           first_hi, first_lo, second_hi, second_lo, rhs_wide, base, zbuf, part_in, part_out, diag_in, diag_out, stack,
           local_sem, slot_send, slot_recv, mat_send, mat_recv, z_send, z_recv, y_send, y_recv, d_send, d_recv, core_done):
    pieces, fold_rows = base.shape[0], base.shape[1]
    own = rhs.shape[1]
    fold = own // fold_rows
    width = LANES // fold
    lane_group = lax.div(iota((fold_rows, LANES), 1), width)
    group = SIDE * SIDE
    span = SIDE * own
    chain = lax.axis_index("chain")
    me = lax.axis_index("tile")
    y, z = me // SIDE, me % SIDE
    not_last = chain < chains - 1
    last = chain == chains - 1
    odd = chain % 2
    across, along = y * odd + z * (1 - odd), z * odd + y * (1 - odd)
    across_step, along_step = 1 + (SIDE - 1) * odd, SIDE - (SIDE - 1) * odd

    def place_of(across_at, along_at):
        return across_at * across_step + along_at * along_step

    def folded(parts):
        result = parts[fold - 1]
        for index in range(fold - 1):
            result = jnp.where(lane_group == index, parts[index], result)
        return result

    def spread(value):
        turns = [value] + [pltpu.roll(value, index * width, 1) for index in range(1, fold)]
        result = []
        for index in range(fold):
            wanted = turns[(fold - 1 - index) % fold]
            for at in range(fold - 1):
                wanted = jnp.where(lane_group == at, turns[(at - index) % fold], wanted)
            result.append(wanted)
        return result

    barrier = pltpu.get_barrier_semaphore()

    def greet(offset, carry):
        pl.semaphore_signal(barrier, inc=1, device_id=(chain, (me + offset) % group), device_id_type=MESH)
        return carry

    lax.fori_loop(1, group, greet, 0)

    @pl.when(not_last)
    def _():
        for row in range(SIDE):
            pl.semaphore_signal(barrier, inc=1, device_id=(chain + 1, place_of(across, row)), device_id_type=MESH)

    @pl.when(chain > 0)
    def _():
        for row in range(SIDE):
            pl.semaphore_signal(barrier, inc=1, device_id=(chain - 1, place_of(row, along)), device_id_type=MESH)

    def load(source, which):
        pltpu.make_async_copy(source, raw, local_sem.at[which]).start()

    def order(ordered, which):
        pltpu.make_async_copy(raw, raw, local_sem.at[which]).wait()
        near = iota((own, LANES), 1) < LANES // 2

        def pair(index, carry):
            for part in range(2):
                for group_at in range(SIDE // 2):
                    begin_at = [pl.multiple_of((2 * group_at + k) * span + index * LANES, LANES) for k in range(2)]
                    one, two = [raw[part, :, pl.ds(at, LANES)] for at in begin_at]
                    lanes = slice(group_at * LANES, (group_at + 1) * LANES)
                    ordered[2 * index, part, :, lanes] = jnp.where(near, one, pltpu.roll(two, LANES // 2, 1))
                    ordered[2 * index + 1, part, :, lanes] = jnp.where(near, pltpu.roll(one, LANES // 2, 1), two)
            return carry

        lax.fori_loop(0, SIDE // 2, pair, 0)

    @pl.when((odd == 1) & not_last)
    def _():
        load(coup, 0)

    @pl.when(last)
    def _():
        load(diag, 0)

    columns, count_rows = upd.shape
    some = width // 2
    wide[columns:] = jnp.zeros_like(wide[columns:])
    rhs_wide[columns:] = jnp.zeros_like(rhs_wide[columns:])
    per_batch = LANES // (2 * width)
    for piece in range(pieces):
        for part in range(2):
            source = (piece // per_batch) * (LANES // 2) + part * (LANES // 4) + (piece % per_batch) * some
            target = piece * width + part * some
            wide[target:target + some] = upd[source:source + some]
            rhs_wide[target:target + some] = rhs[source:source + some]
    row_of = rows[...]
    owner = lax.div(row_of, own)
    local = (row_of - owner * own).astype(F32)
    lane = iota((1, count_rows), 1)
    half = count_rows // 2
    live = jnp.where(lane < half, lane, lane - half) < jnp.where(lane < half, counts[0], counts[1])
    hits = (iota((group, count_rows), 0) == owner).astype(F32)
    before = (iota((count_rows, count_rows), 0) < iota((count_rows, count_rows), 1)).astype(F32).astype(BF16)
    earlier = jnp.dot(hits.astype(BF16), before, preferred_element_type=F32)
    rank = jnp.sum(hits * earlier, axis=0, keepdims=True)
    slot = jnp.where(live, owner.astype(F32) * SLOTS + rank, -1.0)
    pick = iota((group * SLOTS, count_rows), 0).astype(F32) == slot
    place = jnp.sum(jnp.where(pick, local, 0.0), axis=1, keepdims=True)
    pick = pick.astype(F32).astype(BF16)
    by_columns = (((1,), (1,)), ((), ()))
    payload = 0.0
    for part in split(wide[...]):
        payload += lax.dot_general(pick, part, by_columns, preferred_element_type=F32)
    payload = jnp.where(iota(payload.shape, 1) == columns, place, payload)
    slots_out[...] = payload.reshape(slots_out.shape)

    same = (iota((own, own), 0) == iota((own, own), 1)).astype(F32).astype(BF16)
    high, low = split(rhs_wide[...])
    rest = (rhs_wide[...] - high.astype(F32) - low.astype(F32)).astype(BF16)
    rhs_rows = 0.0
    for part in (rest, low, high):
        rhs_rows += lax.dot_general(same, part, by_columns, preferred_element_type=F32)

    @pl.when(odd == 1)
    def _():
        order(sorted_first, 0)

    ends = (chain == 0) | last

    @pl.when(ends)
    def _():
        pl.semaphore_wait(barrier, group - 1 + SIDE)

    @pl.when(jnp.logical_not(ends))
    def _():
        pl.semaphore_wait(barrier, group - 1 + 2 * SIDE)

    def send_slots(offset, carry):
        peer = (me + offset) % group
        remote(slots_out.at[peer], slots_in.at[me], slot_send, slot_recv, (chain, peer)).start()
        return carry

    def columns_of(source, row):
        return source.at[:, :, pl.ds(pl.multiple_of(row * span, span), span)]

    def send_even(source, target, which):
        pltpu.make_async_copy(columns_of(source, along), target.at[along], local_sem.at[which]).start()
        for offset in (4, 3, 5, 2, 6, 1, 7):
            row = (along + offset) % SIDE
            remote(columns_of(source, row), target.at[along], mat_send.at[which], mat_recv.at[which],
                   (chain, place_of(across, row))).start()

    def send_odd(ordered, target, which):
        pltpu.make_async_copy(ordered.at[along], target.at[along], local_sem.at[which]).start()
        for offset in (4, 3, 5, 2, 6, 1, 7):
            row = (along + offset) % SIDE
            remote(ordered.at[row], target.at[along], mat_send.at[which], mat_recv.at[which],
                   (chain, place_of(across, row))).start()

    def take_matrix(target, which, hi, lo):
        pltpu.make_async_copy(target.at[along], target.at[along], local_sem.at[which]).wait()
        seven = target.at[pl.ds(0, SIDE - 1)]
        remote(seven, seven, mat_send.at[which], mat_recv.at[which], (chain, me)).wait_recv()

        shift = (SIDE + 2 - across) % SIDE * own
        half_span = span // 2

        def cut(row, carry):
            for part in range(2):
                high, low = split(pltpu.roll(target[row, part], shift, 1))
                at = pl.ds(pl.multiple_of(row * own, own), own)
                for side in range(2):
                    here = side * span + part * half_span
                    hi[at, here:here + half_span] = high[:, side * half_span:(side + 1) * half_span]
                    lo[at, here:here + half_span] = low[:, side * half_span:(side + 1) * half_span]
            return carry

        lax.fori_loop(0, SIDE, cut, 0)

    lax.fori_loop(1, group, send_slots, 0)
    slots_in[me] = slots_out[me]

    @pl.when(odd == 0)
    def _():
        send_even(coup, first, 0)

    @pl.when(odd == 1)
    def _():
        send_odd(sorted_first, first, 0)

    most = slots_in.at[pl.ds(0, group - 1)]
    remote(most, most, slot_send, slot_recv, (chain, me)).wait_recv()
    arrived = slots_in[...].reshape(group * SLOTS, slots_in.shape[2])
    pick = (arrived[:, columns:columns + 1] == iota((group * SLOTS, own), 1).astype(F32)).astype(F32).astype(BF16)
    high, low = split(arrived)
    by_rows = (((0,), (0,)), ((), ()))
    total = (lax.dot_general(pick, high, by_rows, preferred_element_type=F32)
             + lax.dot_general(pick, low, by_rows, preferred_element_type=F32))
    total = rhs_rows - total
    for piece in range(pieces):
        column = piece * width
        tile = total[:, column // LANES * LANES:column // LANES * LANES + LANES]
        parts = []
        for index in range(fold):
            turn = (index * width - column) % LANES
            part = tile[index * fold_rows:(index + 1) * fold_rows]
            parts.append(pltpu.roll(part, turn, 1) if turn else part)
        base[piece] = folded(parts)

    def send_second():
        @pl.when(odd == 0)
        def _():
            send_even(diag, second, 1)

        @pl.when((odd == 1) & not_last)
        def _():
            load(diag, 1)
            order(sorted_second, 1)
            send_odd(sorted_second, second, 1)

    def begin(piece):
        @pl.when(chain == 0)
        def _():
            zbuf[piece, across] = base[piece]

        @pl.when(chain > 0)
        def _():
            remote(part_in.at[piece], part_in.at[piece], y_send.at[piece], y_recv.at[piece], (chain, me)).wait_recv()
            zbuf[piece, across] = base[piece] - jnp.sum(part_in[piece], axis=0)

        for offset in (4, 3, 5, 2, 6, 1, 7):
            peer = (across + offset) % SIDE
            side = 0 if offset in (1, 2, 7) else 1
            remote(zbuf.at[piece, across], zbuf.at[piece, across], z_send.at[piece], z_recv.at[piece, side],
                   (chain, place_of(peer, along))).start()

    @pl.when(chain == 0)
    def _():
        def start(piece, carry):
            begin(piece)
            return carry

        lax.fori_loop(0, pieces, start, 0)

    take_matrix(first, 0, first_hi, first_lo)

    late = chain < chains // 2

    @pl.when(jnp.logical_not(late))
    def _():
        send_second()

    def product(hi, lo, both):
        wide_sum = jnp.dot(hi, both, preferred_element_type=F32)
        narrow = jnp.dot(lo, both[:, :LANES], preferred_element_type=F32)
        return wide_sum[:, :LANES] + wide_sum[:, LANES:] + narrow

    def store(piece, sums, target):
        for row in range(SIDE):
            target[piece, row] = folded(
                [sums[row * own + at * fold_rows:row * own + (at + 1) * fold_rows] for at in range(fold)])

    def send_diag(piece, source):
        diag_in[piece, along] = source[piece, along]
        for offset in (4, 3, 5, 2, 6, 1, 7):
            row = (along + offset) % SIDE
            remote(source.at[piece, row], diag_in.at[piece, along], d_send.at[piece], d_recv.at[piece],
                   (chain, place_of(across, row))).start()

    def finish(piece):
        lane = iota((fold_rows, LANES), 1)
        imag = lane % width >= some
        sums = 0.0
        for side in range(2):
            some_blocks = zbuf.at[piece, pl.ds(0, 3 + side)]
            remote(some_blocks, some_blocks, z_send.at[piece], z_recv.at[piece, side], (chain, me)).wait_recv()
            for near in range(SIDE // 2):
                block = zbuf[piece, (across + side * (SIDE // 2) + near + SIDE - 2) % SIDE]
                turned = jnp.where(imag, pltpu.roll(block, some, 1), -pltpu.roll(block, LANES - some, 1))
                for part, value in enumerate((block, turned)):
                    for index, wanted in enumerate(spread(value)):
                        high, low = split(wanted)
                        at = side * span + part * (span // 2) + near * own + index * fold_rows
                        stack[piece, at:at + fold_rows, :LANES] = high
                        stack[piece, at:at + fold_rows, LANES:] = low
            at = slice(side * span, (side + 1) * span)
            sums = sums + product(first_hi[:, at], first_lo[:, at], stack[piece, at])
        store(piece, sums, part_out)

        @pl.when(not_last)
        def _():
            for offset in (4, 3, 5, 2, 6, 1, 7, 0):
                row = (along + offset) % SIDE
                remote(part_out.at[piece, row], part_in.at[piece, along], y_send.at[piece], y_recv.at[piece],
                       (chain + 1, place_of(across, row))).start()

        @pl.when(last)
        def _():
            send_diag(piece, part_out)

    def step(index, carry):
        @pl.when((index < pieces) & (chain > 0))
        def _():
            begin(index)

        @pl.when(index >= AHEAD)
        def _():
            finish(index - AHEAD)

        return carry

    lax.fori_loop(0, pieces + AHEAD, step, 0)

    @pl.when(late & (odd == 1))
    def _():
        pl.semaphore_signal(core_done, inc=1, device_id=(chain - 1, me), device_id_type=MESH)
        send_second()

    @pl.when(late & (odd == 0))
    def _():
        pl.semaphore_wait(core_done, 1)
        send_second()

    @pl.when(not_last)
    def _():
        take_matrix(second, 1, second_hi, second_lo)

        def solve(piece, carry):
            store(piece, product(second_hi[...], second_lo[...], stack[piece]), diag_out)
            send_diag(piece, diag_out)
            return carry

        lax.fori_loop(0, pieces, solve, 0)

    def collect(piece, carry):
        seven = diag_in.at[piece, pl.ds(0, SIDE - 1)]
        remote(seven, seven, d_send.at[piece], d_recv.at[piece], (chain, me)).wait_recv()
        out[piece] = jnp.sum(diag_in[piece], axis=0)
        return carry

    lax.fori_loop(0, pieces, collect, 0)

    remote(most, most, slot_send, slot_recv, (chain, me)).wait_send()
    seven = first.at[pl.ds(0, SIDE - 1)]
    remote(seven, seven, mat_send.at[0], mat_recv.at[0], (chain, me)).wait_send()

    @pl.when(not_last)
    def _():
        seven = second.at[pl.ds(0, SIDE - 1)]
        remote(seven, seven, mat_send.at[1], mat_recv.at[1], (chain, me)).wait_send()

    def drain(piece, carry):
        seven = zbuf.at[piece, pl.ds(0, SIDE - 1)]
        remote(seven, seven, z_send.at[piece], z_recv.at[piece, 0], (chain, me)).wait_send()
        seven = diag_out.at[piece, pl.ds(0, SIDE - 1)]
        remote(seven, seven, d_send.at[piece], d_recv.at[piece], (chain, me)).wait_send()

        @pl.when(not_last)
        def _():
            remote(part_out.at[piece], part_out.at[piece], y_send.at[piece], y_recv.at[piece], (chain, me)).wait_send()

        return carry

    lax.fori_loop(0, pieces, drain, 0)


def body(chains, right_side, diag_inverse, coupling, updates, update_rows, tile_counts):
    batches, halves, sources, own = right_side.shape
    fold = FOLD
    fold_rows, width = own // fold, LANES // fold
    pieces = batches * halves * sources // width
    group = SIDE * SIDE
    span = SIDE * own
    count_rows = updates.shape[0]
    vmem = pl.BlockSpec(memory_space=pltpu.VMEM)
    hbm = pl.BlockSpec(memory_space=pltpu.HBM)
    block = (pieces, SIDE, fold_rows, LANES)
    dma = pltpu.SemaphoreType.DMA
    solved = pl.pallas_call(
        functools.partial(kernel, chains),
        out_shape=jax.ShapeDtypeStruct((pieces, fold_rows, LANES), F32),
        in_specs=[vmem, vmem, vmem, pl.BlockSpec(memory_space=pltpu.SMEM), hbm, hbm],
        out_specs=vmem,
        scratch_shapes=[
            pltpu.VMEM((2 * LANES, count_rows), F32),
            pltpu.VMEM((group, SLOTS, 2 * LANES), F32),
            pltpu.VMEM((group, SLOTS, 2 * LANES), F32),
            pltpu.VMEM((2, own, group * own), F32),
            pltpu.VMEM((SIDE, 2, own, span), F32),
            pltpu.VMEM((SIDE, 2, own, span), F32),
            pltpu.VMEM((SIDE, 2, own, span), F32),
            pltpu.VMEM((SIDE, 2, own, span), F32),
            pltpu.VMEM((span, 2 * span), BF16),
            pltpu.VMEM((span, 2 * span), BF16),
            pltpu.VMEM((span, 2 * span), BF16),
            pltpu.VMEM((span, 2 * span), BF16),
            pltpu.VMEM((2 * LANES, own), F32),
            pltpu.VMEM((pieces, fold_rows, LANES), F32),
            pltpu.VMEM(block, F32),
            pltpu.VMEM(block, F32),
            pltpu.VMEM(block, F32),
            pltpu.VMEM(block, F32),
            pltpu.VMEM(block, F32),
            pltpu.VMEM((pieces, 2 * span, 2 * LANES), BF16),
            dma((2,)),
            dma,
            dma,
            dma((2,)),
            dma((2,)),
            dma((pieces,)),
            dma((pieces, 2)),
            dma((pieces,)),
            dma((pieces,)),
            dma((pieces,)),
            dma((pieces,)),
            pltpu.SemaphoreType.REGULAR,
        ],
        compiler_params=pltpu.CompilerParams(collective_id=0, has_side_effects=True, vmem_limit_bytes=63 << 20),
    )(right_side.reshape(batches * halves * sources, own), updates.T, update_rows.reshape(1, count_rows), tile_counts, diag_inverse, coupling)
    solved = solved.reshape(batches, pieces // batches, fold_rows, fold, halves, width // halves)
    return solved.transpose(0, 4, 1, 5, 3, 2).reshape(right_side.shape)


def solution(mesh):
    in_specs = (
        P(None, None, None, ("chain", "tile")),
        P(None, ("chain", "tile"), None),
        P(None, ("chain", "tile"), None),
        P(("chain", "tile"), None),
        P(("chain", "tile")),
        P(("chain", "tile")),
    )
    out_specs = P(None, None, None, ("chain", "tile"))
    run = functools.partial(body, mesh.shape["chain"])
    return jax.shard_map(run, mesh=mesh, in_specs=in_specs, out_specs=out_specs, check_vma=False)
```

```python
import functools

import jax
import jax.numpy as jnp
from jax import lax
from jax.experimental import pallas as pl
from jax.experimental.pallas import tpu as pltpu
from jax.sharding import PartitionSpec as P

MESH = pl.DeviceIdType.MESH
F32 = jnp.float32
BF16 = jnp.bfloat16
SIDE = 8
FOLD = 4
AHEAD = 3
SLOTS = 8
LANES = 128


def remote(src, dst, send_sem, recv_sem, device):
    return pltpu.make_async_remote_copy(
        src_ref=src, dst_ref=dst, send_sem=send_sem, recv_sem=recv_sem, device_id=device, device_id_type=MESH
    )


def split(value):
    high = value.astype(BF16)
    return high, (value - high.astype(F32)).astype(BF16)


def iota(shape, axis):
    return lax.broadcasted_iota(jnp.int32, shape, axis)


def kernel(chains, rhs, upd, rows, counts, diag, coup, out, wide, slots_out, slots_in, raw, sorted_first, sorted_second, first, second,
           first_hi, first_lo, second_hi, second_lo, rhs_wide, base, zbuf, part_in, part_out, diag_in, diag_out, stack,
           local_sem, slot_send, slot_recv, mat_send, mat_recv, z_send, z_recv, y_send, y_recv, d_send, d_recv, core_done):
    pieces, fold_rows = base.shape[0], base.shape[1]
    own = rhs.shape[1]
    fold = own // fold_rows
    width = LANES // fold
    lane_group = lax.div(iota((fold_rows, LANES), 1), width)
    group = SIDE * SIDE
    span = SIDE * own
    chain = lax.axis_index("chain")
    me = lax.axis_index("tile")
    y, z = me // SIDE, me % SIDE
    not_last = chain < chains - 1
    last = chain == chains - 1
    odd = chain % 2
    across, along = y * odd + z * (1 - odd), z * odd + y * (1 - odd)
    across_step, along_step = 1 + (SIDE - 1) * odd, SIDE - (SIDE - 1) * odd

    def place_of(across_at, along_at):
        return across_at * across_step + along_at * along_step

    def folded(parts):
        result = parts[fold - 1]
        for index in range(fold - 1):
            result = jnp.where(lane_group == index, parts[index], result)
        return result

    def spread(value):
        turns = [value] + [pltpu.roll(value, index * width, 1) for index in range(1, fold)]
        result = []
        for index in range(fold):
            wanted = turns[(fold - 1 - index) % fold]
            for at in range(fold - 1):
                wanted = jnp.where(lane_group == at, turns[(at - index) % fold], wanted)
            result.append(wanted)
        return result

    barrier = pltpu.get_barrier_semaphore()

    def greet(offset, carry):
        pl.semaphore_signal(barrier, inc=1, device_id=(chain, (me + offset) % group), device_id_type=MESH)
        return carry

    lax.fori_loop(1, group, greet, 0)

    @pl.when(not_last)
    def _():
        for row in range(SIDE):
            pl.semaphore_signal(barrier, inc=1, device_id=(chain + 1, place_of(across, row)), device_id_type=MESH)

    @pl.when(chain > 0)
    def _():
        for row in range(SIDE):
            pl.semaphore_signal(barrier, inc=1, device_id=(chain - 1, place_of(row, along)), device_id_type=MESH)

    def load(source, which):
        pltpu.make_async_copy(source, raw, local_sem.at[which]).start()

    def order(ordered, which):
        pltpu.make_async_copy(raw, raw, local_sem.at[which]).wait()
        near = iota((own, LANES), 1) < LANES // 2

        def pair(index, carry):
            for part in range(2):
                for group_at in range(SIDE // 2):
                    begin_at = [pl.multiple_of((2 * group_at + k) * span + index * LANES, LANES) for k in range(2)]
                    one, two = [raw[part, :, pl.ds(at, LANES)] for at in begin_at]
                    lanes = slice(group_at * LANES, (group_at + 1) * LANES)
                    ordered[2 * index, part, :, lanes] = jnp.where(near, one, pltpu.roll(two, LANES // 2, 1))
                    ordered[2 * index + 1, part, :, lanes] = jnp.where(near, pltpu.roll(one, LANES // 2, 1), two)
            return carry

        lax.fori_loop(0, SIDE // 2, pair, 0)

    @pl.when((odd == 1) & not_last)
    def _():
        load(coup, 0)

    @pl.when(last)
    def _():
        load(diag, 0)

    columns, count_rows = upd.shape
    some = width // 2
    wide[columns:] = jnp.zeros_like(wide[columns:])
    rhs_wide[columns:] = jnp.zeros_like(rhs_wide[columns:])
    per_batch = LANES // (2 * width)
    for piece in range(pieces):
        for part in range(2):
            source = (piece // per_batch) * (LANES // 2) + part * (LANES // 4) + (piece % per_batch) * some
            target = piece * width + part * some
            wide[target:target + some] = upd[source:source + some]
            rhs_wide[target:target + some] = rhs[source:source + some]
    row_of = rows[...]
    owner = lax.div(row_of, own)
    local = (row_of - owner * own).astype(F32)
    lane = iota((1, count_rows), 1)
    half = count_rows // 2
    live = jnp.where(lane < half, lane, lane - half) < jnp.where(lane < half, counts[0], counts[1])
    hits = (iota((group, count_rows), 0) == owner).astype(F32)
    before = (iota((count_rows, count_rows), 0) < iota((count_rows, count_rows), 1)).astype(F32).astype(BF16)
    earlier = jnp.dot(hits.astype(BF16), before, preferred_element_type=F32)
    rank = jnp.sum(hits * earlier, axis=0, keepdims=True)
    slot = jnp.where(live, owner.astype(F32) * SLOTS + rank, -1.0)
    pick = iota((group * SLOTS, count_rows), 0).astype(F32) == slot
    place = jnp.sum(jnp.where(pick, local, 0.0), axis=1, keepdims=True)
    pick = pick.astype(F32).astype(BF16)
    by_columns = (((1,), (1,)), ((), ()))
    payload = 0.0
    for part in split(wide[...]):
        payload += lax.dot_general(pick, part, by_columns, preferred_element_type=F32)
    payload = jnp.where(iota(payload.shape, 1) == columns, place, payload)
    slots_out[...] = payload.reshape(slots_out.shape)

    same = (iota((own, own), 0) == iota((own, own), 1)).astype(F32).astype(BF16)
    high, low = split(rhs_wide[...])
    rest = (rhs_wide[...] - high.astype(F32) - low.astype(F32)).astype(BF16)
    rhs_rows = 0.0
    for part in (rest, low, high):
        rhs_rows += lax.dot_general(same, part, by_columns, preferred_element_type=F32)

    @pl.when(odd == 1)
    def _():
        order(sorted_first, 0)

    ends = (chain == 0) | last

    @pl.when(ends)
    def _():
        pl.semaphore_wait(barrier, group - 1 + SIDE)

    @pl.when(jnp.logical_not(ends))
    def _():
        pl.semaphore_wait(barrier, group - 1 + 2 * SIDE)

    def send_slots(offset, carry):
        peer = (me + offset) % group
        remote(slots_out.at[peer], slots_in.at[me], slot_send, slot_recv, (chain, peer)).start()
        return carry

    def columns_of(source, row):
        return source.at[:, :, pl.ds(pl.multiple_of(row * span, span), span)]

    def send_even(source, target, which):
        pltpu.make_async_copy(columns_of(source, along), target.at[along], local_sem.at[which]).start()
        for offset in (4, 3, 5, 2, 6, 1, 7):
            row = (along + offset) % SIDE
            remote(columns_of(source, row), target.at[along], mat_send.at[which], mat_recv.at[which],
                   (chain, place_of(across, row))).start()

    def send_odd(ordered, target, which):
        pltpu.make_async_copy(ordered.at[along], target.at[along], local_sem.at[which]).start()
        for offset in (4, 3, 5, 2, 6, 1, 7):
            row = (along + offset) % SIDE
            remote(ordered.at[row], target.at[along], mat_send.at[which], mat_recv.at[which],
                   (chain, place_of(across, row))).start()

    def take_matrix(target, which, hi, lo):
        pltpu.make_async_copy(target.at[along], target.at[along], local_sem.at[which]).wait()
        seven = target.at[pl.ds(0, SIDE - 1)]
        remote(seven, seven, mat_send.at[which], mat_recv.at[which], (chain, me)).wait_recv()

        shift = (SIDE + 2 - across) % SIDE * own
        half_span = span // 2

        def cut(row, carry):
            for part in range(2):
                high, low = split(pltpu.roll(target[row, part], shift, 1))
                at = pl.ds(pl.multiple_of(row * own, own), own)
                for side in range(2):
                    here = side * span + part * half_span
                    hi[at, here:here + half_span] = high[:, side * half_span:(side + 1) * half_span]
                    lo[at, here:here + half_span] = low[:, side * half_span:(side + 1) * half_span]
            return carry

        lax.fori_loop(0, SIDE, cut, 0)

    slots_in[me] = slots_out[me]

    @pl.when(odd == 0)
    def _():
        lax.fori_loop(1, group, send_slots, 0)
        send_even(coup, first, 0)

    @pl.when(odd == 1)
    def _():
        send_odd(sorted_first, first, 0)
        lax.fori_loop(1, group, send_slots, 0)

    most = slots_in.at[pl.ds(0, group - 1)]
    remote(most, most, slot_send, slot_recv, (chain, me)).wait_recv()
    arrived = slots_in[...].reshape(group * SLOTS, slots_in.shape[2])
    pick = (arrived[:, columns:columns + 1] == iota((group * SLOTS, own), 1).astype(F32)).astype(F32).astype(BF16)
    high, low = split(arrived)
    by_rows = (((0,), (0,)), ((), ()))
    total = (lax.dot_general(pick, high, by_rows, preferred_element_type=F32)
             + lax.dot_general(pick, low, by_rows, preferred_element_type=F32))
    total = rhs_rows - total
    for piece in range(pieces):
        column = piece * width
        tile = total[:, column // LANES * LANES:column // LANES * LANES + LANES]
        parts = []
        for index in range(fold):
            turn = (index * width - column) % LANES
            part = tile[index * fold_rows:(index + 1) * fold_rows]
            parts.append(pltpu.roll(part, turn, 1) if turn else part)
        base[piece] = folded(parts)

    def send_second():
        @pl.when(odd == 0)
        def _():
            send_even(diag, second, 1)

        @pl.when((odd == 1) & not_last)
        def _():
            load(diag, 1)
            order(sorted_second, 1)
            send_odd(sorted_second, second, 1)

    def begin(piece):
        @pl.when(chain == 0)
        def _():
            zbuf[piece, across] = base[piece]

        @pl.when(chain > 0)
        def _():
            remote(part_in.at[piece], part_in.at[piece], y_send.at[piece], y_recv.at[piece], (chain, me)).wait_recv()
            zbuf[piece, across] = base[piece] - jnp.sum(part_in[piece], axis=0)

        for offset in (4, 3, 5, 2, 6, 1, 7):
            peer = (across + offset) % SIDE
            side = 0 if offset in (1, 2, 7) else 1
            remote(zbuf.at[piece, across], zbuf.at[piece, across], z_send.at[piece], z_recv.at[piece, side],
                   (chain, place_of(peer, along))).start()

    @pl.when(chain == 0)
    def _():
        def start(piece, carry):
            begin(piece)
            return carry

        lax.fori_loop(0, pieces, start, 0)

    take_matrix(first, 0, first_hi, first_lo)

    late = chain < chains // 2

    @pl.when(jnp.logical_not(late))
    def _():
        send_second()

    def product(hi, lo, both):
        wide_sum = jnp.dot(hi, both, preferred_element_type=F32)
        narrow = jnp.dot(lo, both[:, :LANES], preferred_element_type=F32)
        return wide_sum[:, :LANES] + wide_sum[:, LANES:] + narrow

    def store(piece, sums, target):
        for row in range(SIDE):
            target[piece, row] = folded(
                [sums[row * own + at * fold_rows:row * own + (at + 1) * fold_rows] for at in range(fold)])

    def send_diag(piece, source):
        diag_in[piece, along] = source[piece, along]
        for offset in (4, 3, 5, 2, 6, 1, 7):
            row = (along + offset) % SIDE
            remote(source.at[piece, row], diag_in.at[piece, along], d_send.at[piece], d_recv.at[piece],
                   (chain, place_of(across, row))).start()

    def finish(piece):
        lane = iota((fold_rows, LANES), 1)
        imag = lane % width >= some
        sums = 0.0
        for side in range(2):
            some_blocks = zbuf.at[piece, pl.ds(0, 3 + side)]
            remote(some_blocks, some_blocks, z_send.at[piece], z_recv.at[piece, side], (chain, me)).wait_recv()
            for near in range(SIDE // 2):
                block = zbuf[piece, (across + side * (SIDE // 2) + near + SIDE - 2) % SIDE]
                turned = jnp.where(imag, pltpu.roll(block, some, 1), -pltpu.roll(block, LANES - some, 1))
                for part, value in enumerate((block, turned)):
                    for index, wanted in enumerate(spread(value)):
                        high, low = split(wanted)
                        at = side * span + part * (span // 2) + near * own + index * fold_rows
                        stack[piece, at:at + fold_rows, :LANES] = high
                        stack[piece, at:at + fold_rows, LANES:] = low
            at = slice(side * span, (side + 1) * span)
            sums = sums + product(first_hi[:, at], first_lo[:, at], stack[piece, at])
        store(piece, sums, part_out)

        @pl.when(not_last)
        def _():
            for offset in (4, 3, 5, 2, 6, 1, 7, 0):
                row = (along + offset) % SIDE
                remote(part_out.at[piece, row], part_in.at[piece, along], y_send.at[piece], y_recv.at[piece],
                       (chain + 1, place_of(across, row))).start()

        @pl.when(last)
        def _():
            send_diag(piece, part_out)

    def step(index, carry):
        @pl.when((index < pieces) & (chain > 0))
        def _():
            begin(index)

        @pl.when(index >= AHEAD)
        def _():
            finish(index - AHEAD)

        return carry

    lax.fori_loop(0, pieces + AHEAD, step, 0)

    @pl.when(late & (odd == 1))
    def _():
        pl.semaphore_signal(core_done, inc=1, device_id=(chain - 1, me), device_id_type=MESH)
        send_second()

    @pl.when(late & (odd == 0))
    def _():
        pl.semaphore_wait(core_done, 1)
        send_second()

    @pl.when(not_last)
    def _():
        take_matrix(second, 1, second_hi, second_lo)

        def solve(piece, carry):
            store(piece, product(second_hi[...], second_lo[...], stack[piece]), diag_out)
            send_diag(piece, diag_out)
            return carry

        lax.fori_loop(0, pieces, solve, 0)

    def collect(piece, carry):
        seven = diag_in.at[piece, pl.ds(0, SIDE - 1)]
        remote(seven, seven, d_send.at[piece], d_recv.at[piece], (chain, me)).wait_recv()
        out[piece] = jnp.sum(diag_in[piece], axis=0)
        return carry

    lax.fori_loop(0, pieces, collect, 0)

    remote(most, most, slot_send, slot_recv, (chain, me)).wait_send()
    seven = first.at[pl.ds(0, SIDE - 1)]
    remote(seven, seven, mat_send.at[0], mat_recv.at[0], (chain, me)).wait_send()

    @pl.when(not_last)
    def _():
        seven = second.at[pl.ds(0, SIDE - 1)]
        remote(seven, seven, mat_send.at[1], mat_recv.at[1], (chain, me)).wait_send()

    def drain(piece, carry):
        seven = zbuf.at[piece, pl.ds(0, SIDE - 1)]
        remote(seven, seven, z_send.at[piece], z_recv.at[piece, 0], (chain, me)).wait_send()
        seven = diag_out.at[piece, pl.ds(0, SIDE - 1)]
        remote(seven, seven, d_send.at[piece], d_recv.at[piece], (chain, me)).wait_send()

        @pl.when(not_last)
        def _():
            remote(part_out.at[piece], part_out.at[piece], y_send.at[piece], y_recv.at[piece], (chain, me)).wait_send()

        return carry

    lax.fori_loop(0, pieces, drain, 0)


def body(chains, right_side, diag_inverse, coupling, updates, update_rows, tile_counts):
    batches, halves, sources, own = right_side.shape
    fold = FOLD
    fold_rows, width = own // fold, LANES // fold
    pieces = batches * halves * sources // width
    group = SIDE * SIDE
    span = SIDE * own
    count_rows = updates.shape[0]
    vmem = pl.BlockSpec(memory_space=pltpu.VMEM)
    hbm = pl.BlockSpec(memory_space=pltpu.HBM)
    block = (pieces, SIDE, fold_rows, LANES)
    dma = pltpu.SemaphoreType.DMA
    solved = pl.pallas_call(
        functools.partial(kernel, chains),
        out_shape=jax.ShapeDtypeStruct((pieces, fold_rows, LANES), F32),
        in_specs=[vmem, vmem, vmem, pl.BlockSpec(memory_space=pltpu.SMEM), hbm, hbm],
        out_specs=vmem,
        scratch_shapes=[
            pltpu.VMEM((2 * LANES, count_rows), F32),
            pltpu.VMEM((group, SLOTS, 2 * LANES), F32),
            pltpu.VMEM((group, SLOTS, 2 * LANES), F32),
            pltpu.VMEM((2, own, group * own), F32),
            pltpu.VMEM((SIDE, 2, own, span), F32),
            pltpu.VMEM((SIDE, 2, own, span), F32),
            pltpu.VMEM((SIDE, 2, own, span), F32),
            pltpu.VMEM((SIDE, 2, own, span), F32),
            pltpu.VMEM((span, 2 * span), BF16),
            pltpu.VMEM((span, 2 * span), BF16),
            pltpu.VMEM((span, 2 * span), BF16),
            pltpu.VMEM((span, 2 * span), BF16),
            pltpu.VMEM((2 * LANES, own), F32),
            pltpu.VMEM((pieces, fold_rows, LANES), F32),
            pltpu.VMEM(block, F32),
            pltpu.VMEM(block, F32),
            pltpu.VMEM(block, F32),
            pltpu.VMEM(block, F32),
            pltpu.VMEM(block, F32),
            pltpu.VMEM((pieces, 2 * span, 2 * LANES), BF16),
            dma((2,)),
            dma,
            dma,
            dma((2,)),
            dma((2,)),
            dma((pieces,)),
            dma((pieces, 2)),
            dma((pieces,)),
            dma((pieces,)),
            dma((pieces,)),
            dma((pieces,)),
            pltpu.SemaphoreType.REGULAR,
        ],
        compiler_params=pltpu.CompilerParams(collective_id=0, has_side_effects=True, vmem_limit_bytes=63 << 20),
    )(right_side.reshape(batches * halves * sources, own), updates.T, update_rows.reshape(1, count_rows), tile_counts, diag_inverse, coupling)
    solved = solved.reshape(batches, pieces // batches, fold_rows, fold, halves, width // halves)
    return solved.transpose(0, 4, 1, 5, 3, 2).reshape(right_side.shape)


def solution(mesh):
    in_specs = (
        P(None, None, None, ("chain", "tile")),
        P(None, ("chain", "tile"), None),
        P(None, ("chain", "tile"), None),
        P(("chain", "tile"), None),
        P(("chain", "tile")),
        P(("chain", "tile")),
    )
    out_specs = P(None, None, None, ("chain", "tile"))
    run = functools.partial(body, mesh.shape["chain"])
    return jax.shard_map(run, mesh=mesh, in_specs=in_specs, out_specs=out_specs, check_vma=False)
```
